32 devices in a mesh: grp: 2 (over x), gx: 16 (over z, y, core).
Axes of the slice: x: 2, y: 2, z: 4, core: 2. Of those that a mesh axis runs over, the one named last changes fastest.
Arguments:
- voltages: bfloat16 [1024, 143360], P(('grp', 'gx')), parts along dimension 0, may hold values from -6 to 6
- taps: float32 [4, 4096], replicated, may hold values from -3 to 3
- weights: bfloat16 [2, 64, 256, 128], P(None, 'gx'), may hold values from -0.25 to 0.25
- antenna_weight_index: int32 [1024], P(('grp', 'gx')), parts along dimension 0, may hold values from 0 to 255
- flagged: int32 [1024], P(('grp', 'gx')), parts along dimension 0, may hold values 0 or 1
- trials: int32 [256], P(('grp', 'gx')), parts along dimension 0, may hold values from 0 to 63
Outputs:
- dedispersed: float32 [2, 32, 256, 64], P(None, None, ('grp', 'gx')), parts along dimension 2
The draws below stay inside these ranges and needn't reach their ends.
There are 2 independent parts, one for each index of `grp`. The reference program is written for one: setup_inputs(seed, part) draws one part's arguments, and reference() takes and returns one part's arrays. A program takes and returns all parts, laid end to end along the dimension named above; an argument that names none is the same for every part. Nothing has to cross between parts.
All inputs are finite; a program needn't handle non-finite values. No bound on the sum of `flagged` on one device may be relied on, other than what follows from the above.
Results may differ from the reference program's by a relative error of at most 0.009.
Values may be sent and summed in bfloat16 or wider, within the bound.
A program may use at most 64 MiB of HBM per device.

```python
import math
import jax
import jax.numpy as jnp
from jax import lax

FRAME_COUNT = 32
FORWARD_LENGTH = 4096
TAP_COUNT = 4
CH_LO = 1024
WEIGHT_ROWS = 256
ANTENNA_COUNT = 512
CHANNEL_COUNT = 64
BEAM_COUNT = 128
SAMPLE_COUNT = 143360


def place_ends(drawn, key, least, high):
    spot = [jax.random.randint(jax.random.fold_in(key, axis), (), 0, length) for axis, length in enumerate(drawn.shape)]
    widest = drawn.shape.index(max(drawn.shape))
    next_to = spot[:widest] + [(spot[widest] + 1) % drawn.shape[widest]] + spot[widest + 1:]
    return drawn.at[tuple(spot)].set(least).at[tuple(next_to)].set(high)


def steps_of(stream_key, extent, split, least, high):
    loudness, own = 1.0, jax.random.fold_in(stream_key, 6)
    for axis_at, shards_of in split:
        draws = jnp.exp(jax.random.uniform(jax.random.fold_in(own, axis_at), (shards_of,), jnp.float32, least / len(split), high / len(split)))
        loudness = loudness * jnp.repeat(draws, extent[axis_at] // shards_of).reshape([-1 if axis == axis_at else 1 for axis in range(len(extent))])
    return loudness


def gaussian(stream_key, dims, width, most, pieces=(), kind=jnp.bfloat16):
    array = width * jax.random.normal(stream_key, dims, jnp.float32)
    if pieces:
        array = array * steps_of(stream_key, dims, pieces, -0.22, 0.18)
    return jnp.clip(array, -most, most).astype(kind)


def setup_inputs(seed: int = 0, part: int = 0) -> dict:
    key_of = jax.random.split(jax.random.key(seed), 7)
    part_keys = jax.random.split(jax.random.fold_in(key_of[6], part), 7)
    voltages = gaussian(part_keys[0], (ANTENNA_COUNT, SAMPLE_COUNT), 1.0, 6.0, ((0, 16),))
    taps = gaussian(key_of[1], (TAP_COUNT, FORWARD_LENGTH), 0.5, 3.0, (), jnp.float32)
    weights = gaussian(key_of[2], (2, CHANNEL_COUNT, WEIGHT_ROWS, BEAM_COUNT), ANTENNA_COUNT ** -0.5, 0.25, ((1, 16),))
    antenna_weight_index = place_ends(jax.random.randint(part_keys[3], (ANTENNA_COUNT,), 0, WEIGHT_ROWS), jax.random.fold_in(part_keys[3], 1), 0, WEIGHT_ROWS - 1).astype(jnp.int32)
    flagged = place_ends((jax.random.randint(part_keys[4], (ANTENNA_COUNT,), 0, 8) < 1).astype(jnp.int32), jax.random.fold_in(part_keys[4], 1), 0, 1)
    trials = place_ends(jax.random.randint(part_keys[5], (BEAM_COUNT,), 0, 64), jax.random.fold_in(part_keys[5], 1), 0, 63).astype(jnp.int32)
    return dict(voltages=voltages, taps=taps, weights=weights, antenna_weight_index=antenna_weight_index, flagged=flagged, trials=trials)


dm_unit = 0.173


def forward_table(nfft_len, first_bin, kept):
    bins = first_bin + jnp.arange(kept, dtype=jnp.int32)
    samples = jnp.arange(nfft_len, dtype=jnp.int32)
    modulo = (bins[:, None] * samples[None, :]) % nfft_len
    angles = modulo.astype(jnp.float32) * (2.0 * math.pi / nfft_len)
    return jnp.concatenate([jnp.cos(angles), -jnp.sin(angles)], 0).astype(jnp.bfloat16)


def inverse_table(length):
    chans = jnp.arange(length, dtype=jnp.int32)
    modulo = (chans[:, None] * chans[None, :]) % length
    angles = modulo.astype(jnp.float32) * (2.0 * math.pi / length)
    cosine = jnp.cos(angles)
    sine = jnp.sin(angles)
    return jnp.stack([jnp.stack([cosine, sine], 1), jnp.stack([-sine, cosine], 1)], 0).astype(jnp.bfloat16)


def filter_frames(frame_samples, taps):
    frames = frame_samples.shape[1] - taps.shape[0] + 1
    running_sum = jnp.zeros((frame_samples.shape[0], frames, frame_samples.shape[2]), jnp.float32)
    for tap_index in range(taps.shape[0]):
        running_sum = running_sum + taps[tap_index].astype(jnp.float32)[None, None, :] * frame_samples[:, tap_index:tap_index + frames].astype(jnp.float32)
    return running_sum.astype(jnp.bfloat16)


def chirp_apply(beams, trial_ids, chan_start, channel_total):
    chans = (chan_start + jnp.arange(beams.shape[3], dtype=jnp.int32)).astype(jnp.float32) / channel_total
    phase = (-2.0 * math.pi * dm_unit) * (trial_ids.astype(jnp.float32) + 1.0)[:, None] * (chans * chans)[None, :]
    cosine = jnp.cos(phase)[None]
    sine = jnp.sin(phase)[None]
    real_part = beams[0].astype(jnp.float32)
    imag_part = beams[1].astype(jnp.float32)
    return jnp.stack([real_part * cosine - imag_part * sine, real_part * sine + imag_part * cosine]).astype(jnp.bfloat16)


def reference(voltages, taps, weights, antenna_weight_index, flagged, trials):
    highest = lax.Precision.HIGHEST
    fwd = forward_table(FORWARD_LENGTH, CH_LO, CHANNEL_COUNT).astype(jnp.float32)
    channel_keep_mask = (1 - flagged).astype(jnp.float32)
    antenna_group = math.gcd(ANTENNA_COUNT, 64)
    frame_samples = voltages.reshape(ANTENNA_COUNT // antenna_group, antenna_group, FRAME_COUNT + TAP_COUNT - 1, FORWARD_LENGTH)
    kept_channels = channel_keep_mask.reshape(ANTENNA_COUNT // antenna_group, antenna_group)

    def spectrum(item):
        volts, kept = item
        filtered = filter_frames(volts, taps)
        result = jnp.einsum("afn,kn->kfa", filtered.astype(jnp.float32), fwd, precision=highest)
        return (result * (FORWARD_LENGTH ** -0.5) * kept[None, None, :]).astype(jnp.bfloat16)

    partial_outputs = lax.map(spectrum, (frame_samples, kept_channels))
    frame_spectra = jnp.transpose(partial_outputs, (1, 2, 0, 3)).reshape(2, CHANNEL_COUNT, FRAME_COUNT, ANTENNA_COUNT)
    onehot = (antenna_weight_index[:, None] == jnp.arange(WEIGHT_ROWS, dtype=jnp.int32)[None, :]).astype(jnp.float32)
    sums = jnp.einsum("rcfa,at->rcft", frame_spectra.astype(jnp.float32), onehot, precision=highest)
    wfloat = weights.astype(jnp.float32)

    def product(left, right):
        return jnp.einsum("cft,ctb->fbc", left, right, precision=highest)

    real_part = product(sums[0], wfloat[0]) - product(sums[1], wfloat[1])
    imag_part = product(sums[0], wfloat[1]) + product(sums[1], wfloat[0])
    beams = jnp.stack([real_part, imag_part]).astype(jnp.bfloat16)
    chirped = chirp_apply(beams, trials, 0, CHANNEL_COUNT)
    inv = inverse_table(CHANNEL_COUNT).astype(jnp.float32)
    result = jnp.einsum("rfbc,rcsd->sfbd", chirped.astype(jnp.float32), inv, precision=highest)
    return result * (CHANNEL_COUNT ** -0.5)
```

```python
import functools
import math

import jax
import jax.numpy as jnp
import numpy as np
from jax import lax
from jax.experimental import pallas as pl
from jax.experimental.pallas import tpu as pltpu
from jax.sharding import PartitionSpec as P

FRAME_COUNT = 32
FORWARD_LENGTH = 4096
TAP_COUNT = 4
CH_LO = 1024
WEIGHT_ROWS = 256
LANES = 128
DM_UNIT = 0.173
MESH = pl.DeviceIdType.MESH
NT = (((1,), (1,)), ((), ()))


def twiddles(channels, owners):
    local = channels // owners
    kept = (np.arange(owners)[:, None, None] * local + np.arange(local)[None, None, :]) + np.zeros((1, 2, 1), np.int64)
    part = np.zeros((owners, 1, local), np.int64) + np.arange(2)[None, :, None]
    kept, part = kept.reshape(-1, 1), part.reshape(-1, 1)
    coarse = (CH_LO + kept) * (np.arange(FORWARD_LENGTH // LANES) * LANES)[None] % FORWARD_LENGTH
    fine = (CH_LO + kept) * np.arange(LANES)[None] % FORWARD_LENGTH
    unit = 2.0 * math.pi / FORWARD_LENGTH
    ch, sh = np.cos(coarse * unit), np.sin(coarse * unit)
    first = np.where(part == 0, ch, -sh)
    second = np.where(part == 0, -sh, -ch)
    pad = np.zeros((first.shape[0], LANES - 2 * first.shape[1]))
    return (
        np.concatenate([first, second, pad], 1).astype(np.float32),
        np.stack([np.cos(fine * unit), np.sin(fine * unit)]).astype(np.float32),
    )


def inverse_rows(channels, owners):
    local = channels // owners
    chan = (np.arange(owners)[None, :] * local + np.arange(local)[:, None])[:, None, :, None]
    time = np.arange(channels)[None, None, None, :]
    angle = (chan * time % channels) * (2.0 * math.pi / channels)
    cosine, sine = np.cos(angle), np.sin(angle)
    real = np.concatenate([cosine, -sine], 1)
    imag = np.concatenate([sine, cosine], 1)
    return np.concatenate([real, imag], 3).reshape(2 * channels, 2 * channels).astype(jnp.bfloat16)


def spectra_kernel(group, steps, volts, taps, coarse, fine, keep, out, table, tapped):
    step = pl.program_id(0)
    rows = coarse.shape[0]
    antennas = volts.shape[0]
    frames = FRAME_COUNT

    @pl.when(step == 0)
    def _():
        half = FORWARD_LENGTH // LANES
        for tile in range(half):
            span = slice(tile * LANES, (tile + 1) * LANES)
            base = (
                coarse[:, tile : tile + 1] * fine[0]
                + coarse[:, half + tile : half + tile + 1] * fine[1]
            )
            for tap in range(TAP_COUNT):
                table[tap * rows : (tap + 1) * rows, span] = (base * taps[tap : tap + 1, span]).astype(jnp.bfloat16)

    left = jnp.concatenate(
        [volts[:, g * FORWARD_LENGTH : (g + 1) * FORWARD_LENGTH] for g in range(group)], 0
    )
    block = group * antennas
    tapped[pl.ds(pl.multiple_of(step * block, block), block), :] = lax.dot_general(
        left, table[...], NT, preferred_element_type=jnp.float32
    )

    per_tile = LANES // antennas

    def emit(tile):
        for part in range(rows // LANES):
            pieces = []
            for f in range(tile * per_tile, (tile + 1) * per_tile):
                total = None
                for tap in range(TAP_COUNT):
                    term = tapped[
                        (f + tap) * antennas : (f + tap + 1) * antennas,
                        tap * rows + part * LANES : tap * rows + (part + 1) * LANES,
                    ]
                    total = term if total is None else total + term
                pieces.append(total * keep[...])
            turned = jnp.concatenate(pieces, 0).T
            eights = LANES // out.shape[1]
            out[part * eights : (part + 1) * eights, :, tile * LANES : (tile + 1) * LANES] = turned.reshape(
                eights, out.shape[1], LANES
            ).astype(jnp.bfloat16)

    ready = 0
    for at in range(steps):
        done = min(((at + 1) * group - TAP_COUNT + 1) // per_tile, frames // per_tile)
        tiles = range(ready, done)
        ready = done

        @pl.when(step == at)
        def _(tiles=tiles):
            for tile in tiles:
                emit(tile)


def spectra(voltages, taps, flagged, channels, owners):
    antennas = voltages.shape[0]
    total = FRAME_COUNT + TAP_COUNT - 1
    group = 7
    steps = total // group
    rows = 2 * channels
    coarse, fine = twiddles(channels, owners)
    keep = jnp.broadcast_to(
        ((1 - flagged).astype(jnp.float32) * FORWARD_LENGTH ** (-0.5))[:, None], (antennas, LANES)
    )
    local = rows // owners
    whole = lambda shape: pl.BlockSpec(shape, lambda i: (0,) * len(shape))
    return pl.pallas_call(
        functools.partial(spectra_kernel, group, steps),
        grid=(steps,),
        out_shape=jax.ShapeDtypeStruct((owners, local, FRAME_COUNT * antennas), jnp.bfloat16),
        in_specs=[
            pl.BlockSpec((antennas, group * FORWARD_LENGTH), lambda i: (0, i)),
            whole(taps.shape),
            whole(coarse.shape),
            whole(fine.shape),
            whole(keep.shape),
        ],
        out_specs=whole((owners, local, FRAME_COUNT * antennas)),
        scratch_shapes=[
            pltpu.VMEM((TAP_COUNT * rows, FORWARD_LENGTH), jnp.bfloat16),
            pltpu.VMEM((total * antennas, TAP_COUNT * rows), jnp.float32),
        ],
        compiler_params=pltpu.CompilerParams(dimension_semantics=("arbitrary",)),
        name="spectra",
    )(voltages, taps, jnp.asarray(coarse), jnp.asarray(fine), keep)


def beams_kernel(
    n, spec, index, weights, chirp, inverse, out,
    got_index, got_spec, gathered, lined, sending, got_beams, turned,
    send_sems, index_sems, spec_sems, beam_sems,
):
    me = lax.axis_index("gx")
    locals_ = weights.shape[1]
    beam_total = weights.shape[3]
    frames = FRAME_COUNT
    antennas = spec.shape[2] // frames
    quad = LANES // antennas
    parts = 2 * locals_
    beams = sending.shape[1] // 2

    barrier = pltpu.get_barrier_semaphore()
    for d in range(1, n):
        pl.semaphore_signal(barrier, inc=1, device_id={"gx": lax.rem(me + d, n)}, device_id_type=MESH)
    pl.semaphore_wait(barrier, n - 1)

    def copies(which, source, target, sems, per_peer):
        made = []
        for d in range(1, n):
            peer = lax.rem(me + d, n)
            made.append(
                pltpu.make_async_remote_copy(
                    src_ref=source.at[peer] if per_peer else source,
                    dst_ref=target.at[me],
                    send_sem=send_sems.at[which, d],
                    recv_sem=sems.at[d],
                    device_id={"gx": peer},
                    device_id_type=MESH,
                )
            )
        for copy in made:
            copy.start()
        return made

    def arrivals(which, source, target, sems, per_peer):
        for d in range(1, n):
            peer = lax.rem(me + n - d, n)
            pltpu.make_async_remote_copy(
                src_ref=source.at[peer] if per_peer else source,
                dst_ref=target.at[peer],
                send_sem=send_sems.at[which, d],
                recv_sem=sems.at[d],
                device_id={"gx": peer},
                device_id_type=MESH,
            ).wait_recv()

    first = copies(0, index, got_index, index_sems, False)
    second = copies(1, spec, got_spec, spec_sems, True)
    got_index[me] = index[...]
    got_spec[me] = spec[me]

    arrivals(0, index, got_index, index_sems, False)
    lane = lax.broadcasted_iota(jnp.int32, (LANES, LANES), 1)
    lane_row = lax.broadcasted_iota(jnp.int32, (8, LANES), 1)
    for ag in range(n // quad):
        row = got_index[ag * quad]
        for q in range(1, quad):
            row = jnp.where(lane_row // antennas == q, got_index[ag * quad + q], row)
        column = jnp.broadcast_to(row[0:1].astype(jnp.float32), (LANES, LANES)).T
        column = column.astype(jnp.int32)
        onehot = jnp.concatenate(
            [
                jnp.where(column == lane + t * LANES, 1.0, 0.0).astype(jnp.bfloat16)
                for t in range(WEIGHT_ROWS // LANES)
            ],
            1,
        )
        for c in range(locals_):
            for r in range(2):
                gathered[c, ag * LANES : (ag + 1) * LANES, r * beam_total : (r + 1) * beam_total] = jnp.dot(
                    onehot, weights[r, c], preferred_element_type=jnp.float32
                ).astype(jnp.bfloat16)

    arrivals(1, spec, got_spec, spec_sems, True)
    lane_part = lax.broadcasted_iota(jnp.int32, (parts, LANES), 1) // antennas
    for sg in range(n // quad):
        for ft in range(frames // quad):
            pieces = [
                got_spec[sg * quad + s, :, ft * LANES : (ft + 1) * LANES].astype(jnp.float32)
                for s in range(quad)
            ]
            for f in range(quad):
                made = None
                for s in range(quad):
                    piece = pieces[s]
                    if s != f:
                        piece = pltpu.roll(piece, ((s - f) * antennas) % LANES, 1)
                    made = piece if made is None else jnp.where(lane_part == s, piece, made)
                at = (ft * quad + f) * parts
                lined[sg, at : at + parts, :] = made

    real, imag = [], []
    for c in range(locals_):
        left = jnp.concatenate(
            [
                jnp.concatenate(
                    [lined[sg, pl.ds(r * locals_ + c, frames, stride=parts), :] for sg in range(n // quad)], 1
                )
                for r in range(2)
            ],
            0,
        ).astype(jnp.bfloat16)
        both = jnp.dot(left, gathered[c], preferred_element_type=jnp.float32)
        real.append(both[:frames, :beam_total] - both[frames:, beam_total:])
        imag.append(both[:frames, beam_total:] + both[frames:, :beam_total])
    real, imag = jnp.concatenate(real, 0), jnp.concatenate(imag, 0)
    owners = LANES // beams
    for bt in range(beam_total // LANES):
        span = slice(bt * LANES, (bt + 1) * LANES)
        pair = [x[:, span].T.reshape(owners, beams, LANES) for x in (real, imag)]
        sending[bt * owners : (bt + 1) * owners] = jnp.concatenate(pair, 1).astype(jnp.bfloat16)

    third = copies(2, sending, got_beams, beam_sems, True)
    got_beams[me] = sending[me]
    arrivals(2, sending, got_beams, beam_sems, True)

    for s in range(n):
        block = got_beams[s].astype(jnp.float32)
        x, y = block[:beams], block[beams:]
        cosine, sine = chirp[0, s], chirp[1, s]
        turned[pl.ds(s, beams, stride=2 * n), :] = x * cosine - y * sine
        turned[pl.ds(n + s, beams, stride=2 * n), :] = x * sine + y * cosine

    wide = 2 * n
    lines = []
    if wide >= LANES:
        for b in range(beams):
            across = [turned[b * wide + t * LANES : b * wide + (t + 1) * LANES, :].T for t in range(wide // LANES)]
            lines.append(
                jnp.concatenate(
                    [across[t][c * frames : (c + 1) * frames] for c in range(locals_) for t in range(len(across))], 1
                )
            )
    else:
        each = LANES // wide
        place = lax.broadcasted_iota(jnp.int32, (frames, LANES), 1) // wide
        for g in range(beams // each):
            across = turned[g * LANES : (g + 1) * LANES, :].T
            for b in range(each):
                made = None
                for c in range(locals_):
                    piece = across[c * frames : (c + 1) * frames]
                    if b != c:
                        piece = pltpu.roll(piece, ((c - b) * wide) % LANES, 1)
                    made = piece if made is None else jnp.where(place == c, piece, made)
                lines.append(made)
    left = jnp.concatenate(lines, 0).astype(jnp.bfloat16)
    channels = n * locals_
    out[...] = jnp.dot(left, inverse[...], preferred_element_type=jnp.float32) * channels ** (-0.5)

    for copy in first + second + third:
        copy.wait_send()


def per_device(voltages, taps, weights, antenna_weight_index, flagged, trials):
    n = lax.axis_size("gx")
    locals_ = weights.shape[1]
    beam_total = weights.shape[3]
    channels = locals_ * n
    antennas = voltages.shape[0]
    beams = trials.shape[0]
    spec = spectra(voltages, taps, flagged, channels, n)
    index = jnp.broadcast_to(jnp.tile(antenna_weight_index, LANES // antennas)[None], (8, LANES))
    chan = jnp.repeat(jnp.arange(channels, dtype=jnp.int32).reshape(n, locals_), FRAME_COUNT, axis=1)
    chan = chan.astype(jnp.float32) / channels
    phase = (-2.0 * math.pi * DM_UNIT) * (trials.astype(jnp.float32) + 1.0)[None, :, None] * (chan * chan)[:, None, :]
    chirp = jnp.stack([jnp.cos(phase), jnp.sin(phase)])
    inverse = jnp.asarray(inverse_rows(channels, n))
    parts = 2 * locals_
    vmem = pl.BlockSpec(memory_space=pltpu.VMEM)
    result = pl.pallas_call(
        functools.partial(beams_kernel, n),
        out_shape=jax.ShapeDtypeStruct((beams * FRAME_COUNT, 2 * channels), jnp.float32),
        in_specs=[vmem] * 5,
        out_specs=vmem,
        scratch_shapes=[
            pltpu.VMEM((n, 8, LANES), jnp.int32),
            pltpu.VMEM((n, parts, FRAME_COUNT * antennas), jnp.bfloat16),
            pltpu.VMEM((locals_, n * antennas, 2 * beam_total), jnp.bfloat16),
            pltpu.VMEM((n * antennas // LANES, FRAME_COUNT * parts, LANES), jnp.float32),
            pltpu.VMEM((n, 2 * beams, LANES), jnp.bfloat16),
            pltpu.VMEM((n, 2 * beams, LANES), jnp.bfloat16),
            pltpu.VMEM((beams * 2 * n, LANES), jnp.float32),
            pltpu.SemaphoreType.DMA((3, n)),
            pltpu.SemaphoreType.DMA((n,)),
            pltpu.SemaphoreType.DMA((n,)),
            pltpu.SemaphoreType.DMA((n,)),
        ],
        compiler_params=pltpu.CompilerParams(collective_id=0, has_side_effects=True),
        name="beams",
    )(spec, index, weights, chirp, inverse)
    result = result.reshape(beams, FRAME_COUNT, 2, channels)
    return jnp.transpose(result, (2, 1, 0, 3))


def solution(mesh):
    return jax.shard_map(
        per_device,
        mesh=mesh,
        in_specs=(
            P(("grp", "gx"), None),
            P(),
            P(None, "gx", None, None),
            P(("grp", "gx")),
            P(("grp", "gx")),
            P(("grp", "gx")),
        ),
        out_specs=P(None, None, ("grp", "gx"), None),
        check_vma=False,
    )
```

```python
import functools
import math

import jax
import jax.numpy as jnp
import numpy as np
from jax import lax
from jax.experimental import pallas as pl
from jax.experimental.pallas import tpu as pltpu
from jax.sharding import PartitionSpec as P

FRAME_COUNT = 32
FORWARD_LENGTH = 4096
TAP_COUNT = 4
CH_LO = 1024
WEIGHT_ROWS = 256
LANES = 128
DM_UNIT = 0.173
MESH = pl.DeviceIdType.MESH
NT = (((1,), (1,)), ((), ()))


def twiddles(channels, owners):
    local = channels // owners
    kept = (np.arange(owners)[:, None, None] * local + np.arange(local)[None, None, :]) + np.zeros((1, 2, 1), np.int64)
    part = np.zeros((owners, 1, local), np.int64) + np.arange(2)[None, :, None]
    kept, part = kept.reshape(-1, 1), part.reshape(-1, 1)
    coarse = (CH_LO + kept) * (np.arange(FORWARD_LENGTH // LANES) * LANES)[None] % FORWARD_LENGTH
    fine = (CH_LO + kept) * np.arange(LANES)[None] % FORWARD_LENGTH
    unit = 2.0 * math.pi / FORWARD_LENGTH
    ch, sh = np.cos(coarse * unit), np.sin(coarse * unit)
    first = np.where(part == 0, ch, -sh)
    second = np.where(part == 0, -sh, -ch)
    pad = np.zeros((first.shape[0], LANES - 2 * first.shape[1]))
    return (
        np.concatenate([first, second, pad], 1).astype(np.float32),
        np.stack([np.cos(fine * unit), np.sin(fine * unit)]).astype(np.float32),
    )


def inverse_rows(channels, owners):
    local = channels // owners
    chan = (np.arange(owners)[None, :] * local + np.arange(local)[:, None])[:, None, :, None]
    time = np.arange(channels)[None, None, None, :]
    angle = (chan * time % channels) * (2.0 * math.pi / channels)
    cosine, sine = np.cos(angle), np.sin(angle)
    real = np.concatenate([cosine, -sine], 1)
    imag = np.concatenate([sine, cosine], 1)
    return np.stack([real, imag]).reshape(2, 2 * channels, channels).astype(jnp.bfloat16)


GROUP = 7


def kernel(
    n, plan, index, flagged, trials, volts_hbm, taps, coarse, fine, weights_hbm, inverse, out,
    volts, weights, table, tapped, keep, chirp, index_row, spec,
    got_index, got_spec, gathered, lined, sending, got_beams, turned, stacked,
    load_sems, send_sems, index_sems, spec_sems, beam_sems,
):
    me = lax.axis_index("gx")
    rows = coarse.shape[0]
    antennas = volts.shape[0]
    locals_ = weights.shape[1]
    beam_total = weights.shape[3]
    channels = n * locals_
    frames = FRAME_COUNT
    quad = LANES // antennas
    parts = 2 * locals_
    beams = sending.shape[1] // 2
    steps = len(plan)

    loads = []
    for at in range(steps):
        span = pl.ds(at * GROUP * FORWARD_LENGTH, GROUP * FORWARD_LENGTH)
        loads.append(pltpu.make_async_copy(volts_hbm.at[:, span], volts.at[:, span], load_sems.at[at]))
    loads.append(pltpu.make_async_copy(weights_hbm, weights, load_sems.at[steps]))
    for load in loads:
        load.start()

    barrier = pltpu.get_barrier_semaphore()
    for d in range(1, n):
        pl.semaphore_signal(barrier, inc=1, device_id={"gx": lax.rem(me + d, n)}, device_id_type=MESH)

    lane_one = lax.broadcasted_iota(jnp.int32, (1, LANES), 1) % antennas
    row = jnp.zeros((1, LANES), jnp.int32)
    for a in range(antennas):
        row = jnp.where(lane_one == a, index[a], row)
    index_row[...] = row
    antenna = lax.broadcasted_iota(jnp.int32, (antennas, LANES), 0)
    off = jnp.zeros((antennas, LANES), jnp.int32)
    for a in range(antennas):
        off = jnp.where(antenna == a, flagged[a], off)
    keep[...] = (1 - off).astype(jnp.float32) * FORWARD_LENGTH ** (-0.5)

    def copies(which, source, target, sems):
        made = []
        for d in range(1, n):
            peer = lax.rem(me + d, n)
            made.append(
                pltpu.make_async_remote_copy(
                    src_ref=source(peer),
                    dst_ref=target(me),
                    send_sem=send_sems.at[which, d],
                    recv_sem=sems.at[d],
                    device_id={"gx": peer},
                    device_id_type=MESH,
                )
            )
        for copy in made:
            copy.start()
        return made

    def arrivals(which, source, target, sems):
        for d in range(1, n):
            peer = lax.rem(me + n - d, n)
            pltpu.make_async_remote_copy(
                src_ref=source(peer),
                dst_ref=target(peer),
                send_sem=send_sems.at[which, d],
                recv_sem=sems.at[d],
                device_id={"gx": peer},
                device_id_type=MESH,
            ).wait_recv()

    index_args = (steps, lambda p: index_row, lambda p: got_index.at[p], index_sems)
    beam_args = (steps + 1, lambda p: sending.at[p], lambda p: got_beams.at[p], beam_sems)

    def piece_args(at):
        span = pl.ds(plan[at][0] * LANES, (plan[at][1] - plan[at][0]) * LANES)
        return (at, lambda p: spec.at[p, :, span], lambda p: got_spec.at[p, :, span], spec_sems.at[at])

    half = FORWARD_LENGTH // LANES
    for tile in range(half):
        span = slice(tile * LANES, (tile + 1) * LANES)
        base = (
            coarse[:, tile : tile + 1] * fine[0]
            + coarse[:, half + tile : half + tile + 1] * fine[1]
        )
        for tap in range(TAP_COUNT):
            table[tap * rows : (tap + 1) * rows, span] = (base * taps[tap : tap + 1, span]).astype(jnp.bfloat16)

    pl.semaphore_wait(barrier, n - 1)
    started = copies(*index_args)
    got_index[me] = index_row[...]

    def emit(tile):
        for part in range(rows // LANES):
            pieces = []
            for f in range(tile * quad, (tile + 1) * quad):
                total = None
                for tap in range(TAP_COUNT):
                    term = tapped[
                        (f + tap) * antennas : (f + tap + 1) * antennas,
                        tap * rows + part * LANES : tap * rows + (part + 1) * LANES,
                    ]
                    total = term if total is None else total + term
                pieces.append(total * keep[...])
            across = jnp.concatenate(pieces, 0).T
            eights = LANES // parts
            spec[part * eights : (part + 1) * eights, :, tile * LANES : (tile + 1) * LANES] = across.reshape(
                eights, parts, LANES
            ).astype(jnp.bfloat16)

    def gather_weights():
        arrivals(*index_args)
        loads[steps].wait()
        lane = lax.broadcasted_iota(jnp.int32, (LANES, LANES), 1)
        lane_quad = lax.broadcasted_iota(jnp.int32, (1, LANES), 1) // antennas
        for ag in range(n // quad):
            row = got_index[ag * quad]
            for q in range(1, quad):
                row = jnp.where(lane_quad == q, got_index[ag * quad + q], row)
            column = jnp.broadcast_to(row.astype(jnp.float32), (LANES, LANES)).T
            column = column.astype(jnp.int32)
            onehot = jnp.concatenate(
                [
                    jnp.where(column == lane + t * LANES, 1.0, 0.0).astype(jnp.bfloat16)
                    for t in range(WEIGHT_ROWS // LANES)
                ],
                1,
            )
            for c in range(locals_):
                for r in range(2):
                    gathered[
                        c, ag * LANES : (ag + 1) * LANES, r * beam_total : (r + 1) * beam_total
                    ] = jnp.dot(onehot, weights[r, c], preferred_element_type=jnp.float32).astype(jnp.bfloat16)

    def turn():
        beam = lax.broadcasted_iota(jnp.int32, (beams, LANES), 0)
        trial = jnp.zeros((beams, LANES), jnp.int32)
        for b in range(beams):
            trial = jnp.where(beam == b, trials[b], trial)
        scaled = (-2.0 * math.pi * DM_UNIT) * (trial.astype(jnp.float32) + 1.0)
        lane_chan = lax.broadcasted_iota(jnp.int32, (n, beams, LANES), 2) // frames
        owner = lax.broadcasted_iota(jnp.int32, (n, beams, LANES), 0)
        chan = (owner * locals_ + lane_chan).astype(jnp.float32) / channels
        phase = scaled[None] * (chan * chan)
        chirp[0] = jnp.cos(phase)
        chirp[1] = jnp.sin(phase)

    for at in range(steps):
        loads[at].wait()
        left = jnp.concatenate(
            [volts[:, g * FORWARD_LENGTH : (g + 1) * FORWARD_LENGTH] for g in range(at * GROUP, (at + 1) * GROUP)], 0
        )
        block = GROUP * antennas
        tapped[at * block : (at + 1) * block, :] = lax.dot_general(
            left, table[...], NT, preferred_element_type=jnp.float32
        )
        for tile in range(*plan[at]):
            emit(tile)
        started += copies(*piece_args(at))
        if at == steps - 2:
            gather_weights()
        if at == steps - 3:
            turn()
    got_spec[me] = spec[me]

    lane_part = lax.broadcasted_iota(jnp.int32, (parts, LANES), 1) // antennas
    for at in range(steps):
        arrivals(*piece_args(at))
        for sg in range(n // quad):
            for ft in range(*plan[at]):
                pieces = [
                    got_spec[sg * quad + s, :, ft * LANES : (ft + 1) * LANES].astype(jnp.float32)
                    for s in range(quad)
                ]
                for f in range(quad):
                    made = None
                    for s in range(quad):
                        piece = pieces[s]
                        if s != f:
                            piece = pltpu.roll(piece, ((s - f) * antennas) % LANES, 1)
                        made = piece if made is None else jnp.where(lane_part == s, piece, made)
                    to = (ft * quad + f) * parts
                    lined[sg, to : to + parts, :] = made

    real, imag = [], []
    for c in range(locals_):
        left = jnp.concatenate(
            [
                jnp.concatenate(
                    [lined[sg, pl.ds(r * locals_ + c, frames, stride=parts), :] for sg in range(n // quad)], 1
                )
                for r in range(2)
            ],
            0,
        ).astype(jnp.bfloat16)
        both = jnp.dot(left, gathered[c], preferred_element_type=jnp.float32)
        real.append(both[:frames, :beam_total] - both[frames:, beam_total:])
        imag.append(both[:frames, beam_total:] + both[frames:, :beam_total])
    real, imag = jnp.concatenate(real, 0), jnp.concatenate(imag, 0)
    owners = LANES // beams
    for bt in range(beam_total // LANES):
        span = slice(bt * LANES, (bt + 1) * LANES)
        pair = [x[:, span].T.reshape(owners, beams, LANES) for x in (real, imag)]
        sending[bt * owners : (bt + 1) * owners] = jnp.concatenate(pair, 1).astype(jnp.bfloat16)

    started += copies(*beam_args)
    got_beams[me] = sending[me]
    arrivals(*beam_args)

    for s in range(n):
        block = got_beams[s].astype(jnp.float32)
        x, y = block[:beams], block[beams:]
        cosine, sine = chirp[0, s], chirp[1, s]
        turned[pl.ds(s, beams, stride=2 * n), :] = x * cosine - y * sine
        turned[pl.ds(n + s, beams, stride=2 * n), :] = x * sine + y * cosine

    wide = 2 * n
    deep = locals_ * wide // LANES
    if wide >= LANES:
        for b in range(beams):
            for t in range(wide // LANES):
                across = turned[b * wide + t * LANES : b * wide + (t + 1) * LANES, :].T
                for c in range(locals_):
                    stacked[c * (wide // LANES) + t, pl.ds(b, frames, stride=beams), :] = across[
                        c * frames : (c + 1) * frames
                    ]
    else:
        each = LANES // wide
        place = lax.broadcasted_iota(jnp.int32, (frames, LANES), 1) // wide
        for g in range(beams // each):
            across = turned[g * LANES : (g + 1) * LANES, :].T
            for b in range(each):
                for k in range(deep):
                    made = None
                    for slot in range(each):
                        c = k * each + slot
                        piece = across[c * frames : (c + 1) * frames]
                        if b != slot:
                            piece = pltpu.roll(piece, ((slot - b) * wide) % LANES, 1)
                        made = piece if made is None else jnp.where(place == slot, piece, made)
                    stacked[k, pl.ds(g * each + b, frames, stride=beams), :] = made
    left = jnp.concatenate([stacked[k] for k in range(deep)], 1).astype(jnp.bfloat16)
    for s in range(2):
        total = jnp.dot(left, inverse[s], preferred_element_type=jnp.float32) * channels ** (-0.5)
        out[s] = total.reshape(frames, beams, channels)

    for copy in started:
        copy.wait_send()


def per_device(voltages, taps, weights, antenna_weight_index, flagged, trials):
    n = lax.axis_size("gx")
    locals_ = weights.shape[1]
    beam_total = weights.shape[3]
    channels = locals_ * n
    antennas = voltages.shape[0]
    beams = trials.shape[0]
    parts = 2 * locals_
    rows = 2 * channels
    total = FRAME_COUNT + TAP_COUNT - 1
    steps = total // GROUP
    coarse, fine = twiddles(channels, n)
    inverse = inverse_rows(channels, n)
    quad = LANES // antennas
    plan, ready = [], 0
    for at in range(steps):
        done = ((at + 1) * GROUP - TAP_COUNT + 1) // quad
        plan.append((ready, done))
        ready = done
    vmem = pl.BlockSpec(memory_space=pltpu.VMEM)
    smem = pl.BlockSpec(memory_space=pltpu.SMEM)
    hbm = pl.BlockSpec(memory_space=pl.ANY)
    return pl.pallas_call(
        functools.partial(kernel, n, plan),
        out_shape=jax.ShapeDtypeStruct((2, FRAME_COUNT, beams, channels), jnp.float32),
        in_specs=[smem, smem, smem, hbm, vmem, vmem, vmem, hbm, vmem],
        out_specs=vmem,
        scratch_shapes=[
            pltpu.VMEM(voltages.shape, jnp.bfloat16),
            pltpu.VMEM(weights.shape, jnp.bfloat16),
            pltpu.VMEM((TAP_COUNT * rows, FORWARD_LENGTH), jnp.bfloat16),
            pltpu.VMEM((total * antennas, TAP_COUNT * rows), jnp.float32),
            pltpu.VMEM((antennas, LANES), jnp.float32),
            pltpu.VMEM((2, n, beams, LANES), jnp.float32),
            pltpu.VMEM((1, LANES), jnp.int32),
            pltpu.VMEM((n, parts, FRAME_COUNT * antennas), jnp.bfloat16),
            pltpu.VMEM((n, 1, LANES), jnp.int32),
            pltpu.VMEM((n, parts, FRAME_COUNT * antennas), jnp.bfloat16),
            pltpu.VMEM((locals_, n * antennas, 2 * beam_total), jnp.bfloat16),
            pltpu.VMEM((n * antennas // LANES, FRAME_COUNT * parts, LANES), jnp.float32),
            pltpu.VMEM((n, 2 * beams, LANES), jnp.bfloat16),
            pltpu.VMEM((n, 2 * beams, LANES), jnp.bfloat16),
            pltpu.VMEM((beams * 2 * n, LANES), jnp.float32),
            pltpu.VMEM((2 * channels // LANES, FRAME_COUNT * beams, LANES), jnp.float32),
            pltpu.SemaphoreType.DMA((steps + 1,)),
            pltpu.SemaphoreType.DMA((steps + 2, n)),
            pltpu.SemaphoreType.DMA((n,)),
            pltpu.SemaphoreType.DMA((steps, n)),
            pltpu.SemaphoreType.DMA((n,)),
        ],
        compiler_params=pltpu.CompilerParams(collective_id=0, has_side_effects=True),
        name="beamformer",
    )(
        antenna_weight_index, flagged, trials, voltages, taps,
        jnp.asarray(coarse), jnp.asarray(fine), weights, jnp.asarray(inverse),
    )


def solution(mesh):
    return jax.shard_map(
        per_device,
        mesh=mesh,
        in_specs=(
            P(("grp", "gx"), None),
            P(),
            P(None, "gx", None, None),
            P(("grp", "gx")),
            P(("grp", "gx")),
            P(("grp", "gx")),
        ),
        out_specs=P(None, None, ("grp", "gx"), None),
        check_vma=False,
    )
```

```python
import functools
import math

import jax
import jax.numpy as jnp
import numpy as np
from jax import lax
from jax.experimental import pallas as pl
from jax.experimental.pallas import tpu as pltpu
from jax.sharding import PartitionSpec as P

FRAME_COUNT = 32
FORWARD_LENGTH = 4096
TAP_COUNT = 4
CH_LO = 1024
WEIGHT_ROWS = 256
LANES = 128
DM_UNIT = 0.173
MESH = pl.DeviceIdType.MESH
NT = (((1,), (1,)), ((), ()))


def twiddles(channels, owners):
    local = channels // owners
    kept = (np.arange(owners)[:, None, None] * local + np.arange(local)[None, None, :]) + np.zeros((1, 2, 1), np.int64)
    part = np.zeros((owners, 1, local), np.int64) + np.arange(2)[None, :, None]
    kept, part = kept.reshape(-1, 1), part.reshape(-1, 1)
    coarse = (CH_LO + kept) * (np.arange(FORWARD_LENGTH // LANES) * LANES)[None] % FORWARD_LENGTH
    fine = (CH_LO + kept) * np.arange(LANES)[None] % FORWARD_LENGTH
    unit = 2.0 * math.pi / FORWARD_LENGTH
    ch, sh = np.cos(coarse * unit), np.sin(coarse * unit)
    first = np.where(part == 0, ch, -sh)
    second = np.where(part == 0, -sh, -ch)
    pad = np.zeros((first.shape[0], LANES - 2 * first.shape[1]))
    return (
        np.concatenate([first, second, pad], 1).astype(np.float32),
        np.stack([np.cos(fine * unit), np.sin(fine * unit)]).astype(np.float32),
    )


def inverse_rows(channels, owners):
    local = channels // owners
    chan = (np.arange(owners)[None, :] * local + np.arange(local)[:, None])[:, None, :, None]
    time = np.arange(channels)[None, None, None, :]
    angle = (chan * time % channels) * (2.0 * math.pi / channels)
    cosine, sine = np.cos(angle), np.sin(angle)
    real = np.concatenate([cosine, -sine], 1)
    imag = np.concatenate([sine, cosine], 1)
    return np.stack([real, imag]).reshape(2, 2 * channels, channels).astype(jnp.bfloat16)


GROUP = 7


def kernel(
    n, plan, index, flagged, trials, volts_hbm, taps, coarse, fine, weights_hbm, inverse, out,
    volts, weights, table, tapped, keep, chirp, index_row, spec,
    got_index, got_spec, gathered, lined, sending, got_beams, turned, stacked,
    load_sems, send_sems, index_sems, spec_sems, beam_sems,
):
    me = lax.axis_index("gx")
    rows = coarse.shape[0]
    antennas = volts.shape[0]
    locals_ = weights.shape[1]
    beam_total = weights.shape[3]
    channels = n * locals_
    frames = FRAME_COUNT
    quad = LANES // antennas
    parts = 2 * locals_
    beams = sending.shape[1] // 2
    steps = len(plan)

    loads = []
    for at in range(steps):
        span = pl.ds(at * GROUP * FORWARD_LENGTH, GROUP * FORWARD_LENGTH)
        loads.append(pltpu.make_async_copy(volts_hbm.at[:, span], volts.at[:, span], load_sems.at[at]))
    loads.append(pltpu.make_async_copy(weights_hbm, weights, load_sems.at[steps]))
    for load in loads[:2]:
        load.start()

    barrier = pltpu.get_barrier_semaphore()
    for d in range(1, n):
        pl.semaphore_signal(barrier, inc=1, device_id={"gx": lax.rem(me + d, n)}, device_id_type=MESH)

    lane_one = lax.broadcasted_iota(jnp.int32, (1, LANES), 1) % antennas
    row = jnp.zeros((1, LANES), jnp.int32)
    for a in range(antennas):
        row = jnp.where(lane_one == a, index[a], row)
    index_row[...] = row
    antenna = lax.broadcasted_iota(jnp.int32, (antennas, LANES), 0)
    off = jnp.zeros((antennas, LANES), jnp.int32)
    for a in range(antennas):
        off = jnp.where(antenna == a, flagged[a], off)
    keep[...] = (1 - off).astype(jnp.float32) * FORWARD_LENGTH ** (-0.5)

    def copies(which, source, target, sems):
        made = []
        for d in range(1, n):
            peer = lax.rem(me + d, n)
            made.append(
                pltpu.make_async_remote_copy(
                    src_ref=source(peer),
                    dst_ref=target(me),
                    send_sem=send_sems.at[which, d],
                    recv_sem=sems.at[d],
                    device_id={"gx": peer},
                    device_id_type=MESH,
                )
            )
        for copy in made:
            copy.start()
        return made

    def arrivals(which, source, target, sems):
        for d in range(1, n):
            peer = lax.rem(me + n - d, n)
            pltpu.make_async_remote_copy(
                src_ref=source(peer),
                dst_ref=target(peer),
                send_sem=send_sems.at[which, d],
                recv_sem=sems.at[d],
                device_id={"gx": peer},
                device_id_type=MESH,
            ).wait_recv()

    index_args = (steps, lambda p: index_row, lambda p: got_index.at[p], index_sems)
    beam_args = (steps + 1, lambda p: sending.at[p], lambda p: got_beams.at[p], beam_sems)

    def piece_args(at):
        span = pl.ds(plan[at][0] * LANES, (plan[at][1] - plan[at][0]) * LANES)
        return (at, lambda p: spec.at[p, :, span], lambda p: got_spec.at[p, :, span], spec_sems.at[at])

    half = FORWARD_LENGTH // LANES
    for tile in range(half):
        span = slice(tile * LANES, (tile + 1) * LANES)
        base = (
            coarse[:, tile : tile + 1] * fine[0]
            + coarse[:, half + tile : half + tile + 1] * fine[1]
        )
        for tap in range(TAP_COUNT):
            table[tap * rows : (tap + 1) * rows, span] = (base * taps[tap : tap + 1, span]).astype(jnp.bfloat16)

    started = []

    def emit(tile):
        for part in range(rows // LANES):
            pieces = []
            for f in range(tile * quad, (tile + 1) * quad):
                total = None
                for tap in range(TAP_COUNT):
                    term = tapped[
                        (f + tap) * antennas : (f + tap + 1) * antennas,
                        tap * rows + part * LANES : tap * rows + (part + 1) * LANES,
                    ]
                    total = term if total is None else total + term
                pieces.append(total * keep[...])
            across = jnp.concatenate(pieces, 0).T
            eights = LANES // parts
            spec[part * eights : (part + 1) * eights, :, tile * LANES : (tile + 1) * LANES] = across.reshape(
                eights, parts, LANES
            ).astype(jnp.bfloat16)

    def gather_weights():
        arrivals(*index_args)
        loads[steps].wait()
        lane = lax.broadcasted_iota(jnp.int32, (LANES, LANES), 1)
        lane_quad = lax.broadcasted_iota(jnp.int32, (1, LANES), 1) // antennas
        for ag in range(n // quad):
            row = got_index[ag * quad]
            for q in range(1, quad):
                row = jnp.where(lane_quad == q, got_index[ag * quad + q], row)
            column = jnp.broadcast_to(row.astype(jnp.float32), (LANES, LANES)).T
            column = column.astype(jnp.int32)
            onehot = jnp.concatenate(
                [
                    jnp.where(column == lane + t * LANES, 1.0, 0.0).astype(jnp.bfloat16)
                    for t in range(WEIGHT_ROWS // LANES)
                ],
                1,
            )
            for c in range(locals_):
                for r in range(2):
                    gathered[
                        c, ag * LANES : (ag + 1) * LANES, r * beam_total : (r + 1) * beam_total
                    ] = jnp.dot(onehot, weights[r, c], preferred_element_type=jnp.float32).astype(jnp.bfloat16)

    def turn():
        beam = lax.broadcasted_iota(jnp.int32, (beams, LANES), 0)
        trial = jnp.zeros((beams, LANES), jnp.int32)
        for b in range(beams):
            trial = jnp.where(beam == b, trials[b], trial)
        scaled = (-2.0 * math.pi * DM_UNIT) * (trial.astype(jnp.float32) + 1.0)
        lane_chan = lax.broadcasted_iota(jnp.int32, (n, beams, LANES), 2) // frames
        owner = lax.broadcasted_iota(jnp.int32, (n, beams, LANES), 0)
        chan = (owner * locals_ + lane_chan).astype(jnp.float32) / channels
        phase = scaled[None] * (chan * chan)
        chirp[0] = jnp.cos(phase)
        chirp[1] = jnp.sin(phase)

    for at in range(steps):
        loads[at].wait()
        if at + 2 < len(loads):
            loads[at + 2].start()
        left = jnp.concatenate(
            [volts[:, g * FORWARD_LENGTH : (g + 1) * FORWARD_LENGTH] for g in range(at * GROUP, (at + 1) * GROUP)], 0
        )
        block = GROUP * antennas
        tapped[at * block : (at + 1) * block, :] = lax.dot_general(
            left, table[...], NT, preferred_element_type=jnp.float32
        )
        for tile in range(*plan[at]):
            emit(tile)
        if at == 0:
            pl.semaphore_wait(barrier, n - 1)
            started += copies(*index_args)
            got_index[me] = index_row[...]
        started += copies(*piece_args(at))
        if at == steps - 2:
            gather_weights()
        if at == steps - 3:
            turn()
    got_spec[me] = spec[me]

    lane_part = lax.broadcasted_iota(jnp.int32, (parts, LANES), 1) // antennas
    for at in range(steps):
        arrivals(*piece_args(at))
        for sg in range(n // quad):
            for ft in range(*plan[at]):
                pieces = [
                    got_spec[sg * quad + s, :, ft * LANES : (ft + 1) * LANES].astype(jnp.float32)
                    for s in range(quad)
                ]
                for f in range(quad):
                    made = None
                    for s in range(quad):
                        piece = pieces[s]
                        if s != f:
                            piece = pltpu.roll(piece, ((s - f) * antennas) % LANES, 1)
                        made = piece if made is None else jnp.where(lane_part == s, piece, made)
                    to = (ft * quad + f) * parts
                    lined[sg, to : to + parts, :] = made

    real, imag = [], []
    for c in range(locals_):
        left = jnp.concatenate(
            [
                jnp.concatenate(
                    [lined[sg, pl.ds(r * locals_ + c, frames, stride=parts), :] for sg in range(n // quad)], 1
                )
                for r in range(2)
            ],
            0,
        ).astype(jnp.bfloat16)
        both = jnp.dot(left, gathered[c], preferred_element_type=jnp.float32)
        real.append(both[:frames, :beam_total] - both[frames:, beam_total:])
        imag.append(both[:frames, beam_total:] + both[frames:, :beam_total])
    real, imag = jnp.concatenate(real, 0), jnp.concatenate(imag, 0)
    owners = LANES // beams
    for bt in range(beam_total // LANES):
        span = slice(bt * LANES, (bt + 1) * LANES)
        pair = [x[:, span].T.reshape(owners, beams, LANES) for x in (real, imag)]
        sending[bt * owners : (bt + 1) * owners] = jnp.concatenate(pair, 1).astype(jnp.bfloat16)

    started += copies(*beam_args)
    got_beams[me] = sending[me]
    arrivals(*beam_args)

    for s in range(n):
        block = got_beams[s].astype(jnp.float32)
        x, y = block[:beams], block[beams:]
        cosine, sine = chirp[0, s], chirp[1, s]
        turned[pl.ds(s, beams, stride=2 * n), :] = x * cosine - y * sine
        turned[pl.ds(n + s, beams, stride=2 * n), :] = x * sine + y * cosine

    wide = 2 * n
    deep = locals_ * wide // LANES
    if wide >= LANES:
        for b in range(beams):
            for t in range(wide // LANES):
                across = turned[b * wide + t * LANES : b * wide + (t + 1) * LANES, :].T
                for c in range(locals_):
                    stacked[c * (wide // LANES) + t, pl.ds(b, frames, stride=beams), :] = across[
                        c * frames : (c + 1) * frames
                    ]
    else:
        each = LANES // wide
        place = lax.broadcasted_iota(jnp.int32, (frames, LANES), 1) // wide
        for g in range(beams // each):
            across = turned[g * LANES : (g + 1) * LANES, :].T
            for b in range(each):
                for k in range(deep):
                    made = None
                    for slot in range(each):
                        c = k * each + slot
                        piece = across[c * frames : (c + 1) * frames]
                        if b != slot:
                            piece = pltpu.roll(piece, ((slot - b) * wide) % LANES, 1)
                        made = piece if made is None else jnp.where(place == slot, piece, made)
                    stacked[k, pl.ds(g * each + b, frames, stride=beams), :] = made
    left = jnp.concatenate([stacked[k] for k in range(deep)], 1).astype(jnp.bfloat16)
    for s in range(2):
        total = jnp.dot(left, inverse[s], preferred_element_type=jnp.float32) * channels ** (-0.5)
        out[s] = total.reshape(frames, beams, channels)

    for copy in started:
        copy.wait_send()


def per_device(voltages, taps, weights, antenna_weight_index, flagged, trials):
    n = lax.axis_size("gx")
    locals_ = weights.shape[1]
    beam_total = weights.shape[3]
    channels = locals_ * n
    antennas = voltages.shape[0]
    beams = trials.shape[0]
    parts = 2 * locals_
    rows = 2 * channels
    total = FRAME_COUNT + TAP_COUNT - 1
    steps = total // GROUP
    coarse, fine = twiddles(channels, n)
    inverse = inverse_rows(channels, n)
    quad = LANES // antennas
    plan, ready = [], 0
    for at in range(steps):
        done = ((at + 1) * GROUP - TAP_COUNT + 1) // quad
        plan.append((ready, done))
        ready = done
    vmem = pl.BlockSpec(memory_space=pltpu.VMEM)
    smem = pl.BlockSpec(memory_space=pltpu.SMEM)
    hbm = pl.BlockSpec(memory_space=pltpu.HBM)
    return pl.pallas_call(
        functools.partial(kernel, n, plan),
        out_shape=jax.ShapeDtypeStruct((2, FRAME_COUNT, beams, channels), jnp.float32),
        in_specs=[smem, smem, smem, hbm, vmem, vmem, vmem, hbm, vmem],
        out_specs=vmem,
        scratch_shapes=[
            pltpu.VMEM(voltages.shape, jnp.bfloat16),
            pltpu.VMEM(weights.shape, jnp.bfloat16),
            pltpu.VMEM((TAP_COUNT * rows, FORWARD_LENGTH), jnp.bfloat16),
            pltpu.VMEM((total * antennas, TAP_COUNT * rows), jnp.float32),
            pltpu.VMEM((antennas, LANES), jnp.float32),
            pltpu.VMEM((2, n, beams, LANES), jnp.float32),
            pltpu.VMEM((1, LANES), jnp.int32),
            pltpu.VMEM((n, parts, FRAME_COUNT * antennas), jnp.bfloat16),
            pltpu.VMEM((n, 1, LANES), jnp.int32),
            pltpu.VMEM((n, parts, FRAME_COUNT * antennas), jnp.bfloat16),
            pltpu.VMEM((locals_, n * antennas, 2 * beam_total), jnp.bfloat16),
            pltpu.VMEM((n * antennas // LANES, FRAME_COUNT * parts, LANES), jnp.float32),
            pltpu.VMEM((n, 2 * beams, LANES), jnp.bfloat16),
            pltpu.VMEM((n, 2 * beams, LANES), jnp.bfloat16),
            pltpu.VMEM((beams * 2 * n, LANES), jnp.float32),
            pltpu.VMEM((2 * channels // LANES, FRAME_COUNT * beams, LANES), jnp.float32),
            pltpu.SemaphoreType.DMA((steps + 1,)),
            pltpu.SemaphoreType.DMA((steps + 2, n)),
            pltpu.SemaphoreType.DMA((n,)),
            pltpu.SemaphoreType.DMA((steps, n)),
            pltpu.SemaphoreType.DMA((n,)),
        ],
        compiler_params=pltpu.CompilerParams(collective_id=0, has_side_effects=True),
        name="beamformer",
    )(
        antenna_weight_index, flagged, trials, voltages, taps,
        jnp.asarray(coarse), jnp.asarray(fine), weights, jnp.asarray(inverse),
    )


def solution(mesh):
    return jax.shard_map(
        per_device,
        mesh=mesh,
        in_specs=(
            P(("grp", "gx"), None),
            P(),
            P(None, "gx", None, None),
            P(("grp", "gx")),
            P(("grp", "gx")),
            P(("grp", "gx")),
        ),
        out_specs=P(None, None, ("grp", "gx"), None),
        check_vma=False,
    )
```

```python
import functools
import math

import jax
import jax.numpy as jnp
import numpy as np
from jax import lax
from jax.experimental import pallas as pl
from jax.experimental.pallas import tpu as pltpu
from jax.sharding import PartitionSpec as P

FRAME_COUNT = 32
FORWARD_LENGTH = 4096
TAP_COUNT = 4
CH_LO = 1024
WEIGHT_ROWS = 256
LANES = 128
DM_UNIT = 0.173
MESH = pl.DeviceIdType.MESH
NT = (((1,), (1,)), ((), ()))


def twiddles(channels, owners):
    local = channels // owners
    kept = (np.arange(owners)[:, None, None] * local + np.arange(local)[None, None, :]) + np.zeros((1, 2, 1), np.int64)
    part = np.zeros((owners, 1, local), np.int64) + np.arange(2)[None, :, None]
    kept, part = kept.reshape(-1, 1), part.reshape(-1, 1)
    coarse = (CH_LO + kept) * (np.arange(FORWARD_LENGTH // LANES) * LANES)[None] % FORWARD_LENGTH
    fine = (CH_LO + kept) * np.arange(LANES)[None] % FORWARD_LENGTH
    unit = 2.0 * math.pi / FORWARD_LENGTH
    ch, sh = np.cos(coarse * unit), np.sin(coarse * unit)
    first = np.where(part == 0, ch, -sh)
    second = np.where(part == 0, -sh, -ch)
    pad = np.zeros((first.shape[0], LANES - 2 * first.shape[1]))
    return (
        np.concatenate([first, second, pad], 1).astype(np.float32),
        np.stack([np.cos(fine * unit), np.sin(fine * unit)]).astype(np.float32),
    )


def inverse_rows(channels, owners):
    local = channels // owners
    chan = (np.arange(owners)[None, :] * local + np.arange(local)[:, None])[:, None, :, None]
    time = np.arange(channels)[None, None, None, :]
    angle = (chan * time % channels) * (2.0 * math.pi / channels)
    cosine, sine = np.cos(angle), np.sin(angle)
    real = np.concatenate([cosine, -sine], 1)
    imag = np.concatenate([sine, cosine], 1)
    return np.stack([real, imag]).reshape(2, 2 * channels, channels).astype(jnp.bfloat16)


GROUPS = (8, 8, 8, 8, 3)


def kernel(
    n, plan, index, flagged, trials, volts_hbm, taps, coarse, fine, weights_hbm, inverse, out,
    volts, weights, table, tapped, keep, chirp, index_row, spec,
    got_index, got_spec, gathered, lined, sending, got_beams, turned, stacked,
    load_sems, send_sems, index_sems, spec_sems, beam_sems,
):
    me = lax.axis_index("gx")
    rows = coarse.shape[0]
    antennas = volts.shape[0]
    locals_ = weights.shape[1]
    beam_total = weights.shape[3]
    channels = n * locals_
    frames = FRAME_COUNT
    quad = LANES // antennas
    parts = 2 * locals_
    beams = sending.shape[1] // 2
    steps = len(plan)

    loads = []
    for at in range(steps):
        span = pl.ds(sum(GROUPS[:at]) * FORWARD_LENGTH, GROUPS[at] * FORWARD_LENGTH)
        loads.append(pltpu.make_async_copy(volts_hbm.at[:, span], volts.at[:, span], load_sems.at[at]))
    loads.append(pltpu.make_async_copy(weights_hbm, weights, load_sems.at[steps]))
    for load in loads[:2]:
        load.start()

    barrier = pltpu.get_barrier_semaphore()
    for d in range(1, n):
        pl.semaphore_signal(barrier, inc=1, device_id={"gx": lax.rem(me + d, n)}, device_id_type=MESH)

    lane_one = lax.broadcasted_iota(jnp.int32, (1, LANES), 1) % antennas
    row = jnp.zeros((1, LANES), jnp.int32)
    for a in range(antennas):
        row = jnp.where(lane_one == a, index[a], row)
    index_row[...] = row
    antenna = lax.broadcasted_iota(jnp.int32, (antennas, LANES), 0)
    off = jnp.zeros((antennas, LANES), jnp.int32)
    for a in range(antennas):
        off = jnp.where(antenna == a, flagged[a], off)
    keep[...] = (1 - off).astype(jnp.float32) * FORWARD_LENGTH ** (-0.5)

    def copies(which, source, target, sems):
        made = []
        for d in range(1, n):
            peer = lax.rem(me + d, n)
            made.append(
                pltpu.make_async_remote_copy(
                    src_ref=source(peer),
                    dst_ref=target(me),
                    send_sem=send_sems.at[which, d],
                    recv_sem=sems.at[d],
                    device_id={"gx": peer},
                    device_id_type=MESH,
                )
            )
        for copy in made:
            copy.start()
        return made

    def arrivals(which, source, target, sems):
        for d in range(1, n):
            peer = lax.rem(me + n - d, n)
            pltpu.make_async_remote_copy(
                src_ref=source(peer),
                dst_ref=target(peer),
                send_sem=send_sems.at[which, d],
                recv_sem=sems.at[d],
                device_id={"gx": peer},
                device_id_type=MESH,
            ).wait_recv()

    index_args = (steps, lambda p: index_row, lambda p: got_index.at[p], index_sems)
    beam_args = (steps + 1, lambda p: sending.at[p], lambda p: got_beams.at[p], beam_sems)

    def piece_args(at):
        span = pl.ds(plan[at][0] * LANES, (plan[at][1] - plan[at][0]) * LANES)
        return (at, lambda p: spec.at[p, :, span], lambda p: got_spec.at[p, :, span], spec_sems.at[at])

    half = FORWARD_LENGTH // LANES
    for tile in range(half):
        span = slice(tile * LANES, (tile + 1) * LANES)
        base = (
            coarse[:, tile : tile + 1] * fine[0]
            + coarse[:, half + tile : half + tile + 1] * fine[1]
        )
        for tap in range(TAP_COUNT):
            table[tap * rows : (tap + 1) * rows, span] = (base * taps[tap : tap + 1, span]).astype(jnp.bfloat16)

    started = []

    def emit(tile):
        for part in range(rows // LANES):
            pieces = []
            for f in range(tile * quad, (tile + 1) * quad):
                total = None
                for tap in range(TAP_COUNT):
                    term = tapped[
                        (f + tap) * antennas : (f + tap + 1) * antennas,
                        tap * rows + part * LANES : tap * rows + (part + 1) * LANES,
                    ]
                    total = term if total is None else total + term
                pieces.append(total * keep[...])
            across = jnp.concatenate(pieces, 0).T
            eights = LANES // parts
            spec[part * eights : (part + 1) * eights, :, tile * LANES : (tile + 1) * LANES] = across.reshape(
                eights, parts, LANES
            ).astype(jnp.bfloat16)

    def gather_weights():
        arrivals(*index_args)
        loads[steps].wait()
        lane = lax.broadcasted_iota(jnp.int32, (LANES, LANES), 1)
        lane_quad = lax.broadcasted_iota(jnp.int32, (1, LANES), 1) // antennas
        for ag in range(n // quad):
            row = got_index[ag * quad]
            for q in range(1, quad):
                row = jnp.where(lane_quad == q, got_index[ag * quad + q], row)
            column = jnp.broadcast_to(row.astype(jnp.float32), (LANES, LANES)).T
            column = column.astype(jnp.int32)
            onehot = jnp.concatenate(
                [
                    jnp.where(column == lane + t * LANES, 1.0, 0.0).astype(jnp.bfloat16)
                    for t in range(WEIGHT_ROWS // LANES)
                ],
                1,
            )
            for c in range(locals_):
                for r in range(2):
                    gathered[
                        c, ag * LANES : (ag + 1) * LANES, r * beam_total : (r + 1) * beam_total
                    ] = jnp.dot(onehot, weights[r, c], preferred_element_type=jnp.float32).astype(jnp.bfloat16)

    def turn():
        beam = lax.broadcasted_iota(jnp.int32, (beams, LANES), 0)
        trial = jnp.zeros((beams, LANES), jnp.int32)
        for b in range(beams):
            trial = jnp.where(beam == b, trials[b], trial)
        scaled = (-2.0 * math.pi * DM_UNIT) * (trial.astype(jnp.float32) + 1.0)
        lane_chan = lax.broadcasted_iota(jnp.int32, (n, beams, LANES), 2) // frames
        owner = lax.broadcasted_iota(jnp.int32, (n, beams, LANES), 0)
        chan = (owner * locals_ + lane_chan).astype(jnp.float32) / channels
        phase = scaled[None] * (chan * chan)
        chirp[0] = jnp.cos(phase)
        chirp[1] = jnp.sin(phase)

    for at in range(steps):
        loads[at].wait()
        if at + 2 < len(loads):
            loads[at + 2].start()
        begin = sum(GROUPS[:at])
        left = jnp.concatenate(
            [volts[:, g * FORWARD_LENGTH : (g + 1) * FORWARD_LENGTH] for g in range(begin, begin + GROUPS[at])], 0
        )
        tapped[begin * antennas : (begin + GROUPS[at]) * antennas, :] = lax.dot_general(
            left, table[...], NT, preferred_element_type=jnp.float32
        )
        for tile in range(*plan[at]):
            emit(tile)
        if at == 0:
            pl.semaphore_wait(barrier, n - 1)
            started += copies(*index_args)
            got_index[me] = index_row[...]
        started += copies(*piece_args(at))
        if at == steps - 2:
            gather_weights()
        if at == steps - 3:
            turn()
    got_spec[me] = spec[me]

    lane_part = lax.broadcasted_iota(jnp.int32, (parts, LANES), 1) // antennas
    for at in range(steps):
        arrivals(*piece_args(at))
        for sg in range(n // quad):
            for ft in range(*plan[at]):
                pieces = [
                    got_spec[sg * quad + s, :, ft * LANES : (ft + 1) * LANES].astype(jnp.float32)
                    for s in range(quad)
                ]
                for f in range(quad):
                    made = None
                    for s in range(quad):
                        piece = pieces[s]
                        if s != f:
                            piece = pltpu.roll(piece, ((s - f) * antennas) % LANES, 1)
                        made = piece if made is None else jnp.where(lane_part == s, piece, made)
                    to = (ft * quad + f) * parts
                    lined[sg, to : to + parts, :] = made

    real, imag = [], []
    for c in range(locals_):
        left = jnp.concatenate(
            [
                jnp.concatenate(
                    [lined[sg, pl.ds(r * locals_ + c, frames, stride=parts), :] for sg in range(n // quad)], 1
                )
                for r in range(2)
            ],
            0,
        ).astype(jnp.bfloat16)
        both = jnp.dot(left, gathered[c], preferred_element_type=jnp.float32)
        real.append(both[:frames, :beam_total] - both[frames:, beam_total:])
        imag.append(both[:frames, beam_total:] + both[frames:, :beam_total])
    real, imag = jnp.concatenate(real, 0), jnp.concatenate(imag, 0)
    owners = LANES // beams
    for bt in range(beam_total // LANES):
        span = slice(bt * LANES, (bt + 1) * LANES)
        pair = [x[:, span].T.reshape(owners, beams, LANES) for x in (real, imag)]
        sending[bt * owners : (bt + 1) * owners] = jnp.concatenate(pair, 1).astype(jnp.bfloat16)

    started += copies(*beam_args)
    got_beams[me] = sending[me]
    arrivals(*beam_args)

    for s in range(n):
        block = got_beams[s].astype(jnp.float32)
        x, y = block[:beams], block[beams:]
        cosine, sine = chirp[0, s], chirp[1, s]
        turned[pl.ds(s, beams, stride=2 * n), :] = x * cosine - y * sine
        turned[pl.ds(n + s, beams, stride=2 * n), :] = x * sine + y * cosine

    wide = 2 * n
    deep = locals_ * wide // LANES
    if wide >= LANES:
        for b in range(beams):
            for t in range(wide // LANES):
                across = turned[b * wide + t * LANES : b * wide + (t + 1) * LANES, :].T
                for c in range(locals_):
                    stacked[c * (wide // LANES) + t, pl.ds(b, frames, stride=beams), :] = across[
                        c * frames : (c + 1) * frames
                    ]
    else:
        each = LANES // wide
        place = lax.broadcasted_iota(jnp.int32, (frames, LANES), 1) // wide
        for g in range(beams // each):
            across = turned[g * LANES : (g + 1) * LANES, :].T
            for b in range(each):
                for k in range(deep):
                    made = None
                    for slot in range(each):
                        c = k * each + slot
                        piece = across[c * frames : (c + 1) * frames]
                        if b != slot:
                            piece = pltpu.roll(piece, ((slot - b) * wide) % LANES, 1)
                        made = piece if made is None else jnp.where(place == slot, piece, made)
                    stacked[k, pl.ds(g * each + b, frames, stride=beams), :] = made
    left = jnp.concatenate([stacked[k] for k in range(deep)], 1).astype(jnp.bfloat16)
    for s in range(2):
        total = jnp.dot(left, inverse[s], preferred_element_type=jnp.float32) * channels ** (-0.5)
        out[s] = total.reshape(frames, beams, channels)

    for copy in started:
        copy.wait_send()


def per_device(voltages, taps, weights, antenna_weight_index, flagged, trials):
    n = lax.axis_size("gx")
    locals_ = weights.shape[1]
    beam_total = weights.shape[3]
    channels = locals_ * n
    antennas = voltages.shape[0]
    beams = trials.shape[0]
    parts = 2 * locals_
    rows = 2 * channels
    total = FRAME_COUNT + TAP_COUNT - 1
    steps = len(GROUPS)
    coarse, fine = twiddles(channels, n)
    inverse = inverse_rows(channels, n)
    quad = LANES // antennas
    plan, ready = [], 0
    for at in range(steps):
        done = (sum(GROUPS[: at + 1]) - TAP_COUNT + 1) // quad
        plan.append((ready, done))
        ready = done
    vmem = pl.BlockSpec(memory_space=pltpu.VMEM)
    smem = pl.BlockSpec(memory_space=pltpu.SMEM)
    hbm = pl.BlockSpec(memory_space=pltpu.HBM)
    return pl.pallas_call(
        functools.partial(kernel, n, plan),
        out_shape=jax.ShapeDtypeStruct((2, FRAME_COUNT, beams, channels), jnp.float32),
        in_specs=[smem, smem, smem, hbm, vmem, vmem, vmem, hbm, vmem],
        out_specs=vmem,
        scratch_shapes=[
            pltpu.VMEM(voltages.shape, jnp.bfloat16),
            pltpu.VMEM(weights.shape, jnp.bfloat16),
            pltpu.VMEM((TAP_COUNT * rows, FORWARD_LENGTH), jnp.bfloat16),
            pltpu.VMEM((total * antennas, TAP_COUNT * rows), jnp.float32),
            pltpu.VMEM((antennas, LANES), jnp.float32),
            pltpu.VMEM((2, n, beams, LANES), jnp.float32),
            pltpu.VMEM((1, LANES), jnp.int32),
            pltpu.VMEM((n, parts, FRAME_COUNT * antennas), jnp.bfloat16),
            pltpu.VMEM((n, 1, LANES), jnp.int32),
            pltpu.VMEM((n, parts, FRAME_COUNT * antennas), jnp.bfloat16),
            pltpu.VMEM((locals_, n * antennas, 2 * beam_total), jnp.bfloat16),
            pltpu.VMEM((n * antennas // LANES, FRAME_COUNT * parts, LANES), jnp.float32),
            pltpu.VMEM((n, 2 * beams, LANES), jnp.bfloat16),
            pltpu.VMEM((n, 2 * beams, LANES), jnp.bfloat16),
            pltpu.VMEM((beams * 2 * n, LANES), jnp.float32),
            pltpu.VMEM((2 * channels // LANES, FRAME_COUNT * beams, LANES), jnp.float32),
            pltpu.SemaphoreType.DMA((steps + 1,)),
            pltpu.SemaphoreType.DMA((steps + 2, n)),
            pltpu.SemaphoreType.DMA((n,)),
            pltpu.SemaphoreType.DMA((steps, n)),
            pltpu.SemaphoreType.DMA((n,)),
        ],
        compiler_params=pltpu.CompilerParams(collective_id=0, has_side_effects=True, vmem_limit_bytes=67043328),
        name="beamformer",
    )(
        antenna_weight_index, flagged, trials, voltages, taps,
        jnp.asarray(coarse), jnp.asarray(fine), weights, jnp.asarray(inverse),
    )


def solution(mesh):
    return jax.shard_map(
        per_device,
        mesh=mesh,
        in_specs=(
            P(("grp", "gx"), None),
            P(),
            P(None, "gx", None, None),
            P(("grp", "gx")),
            P(("grp", "gx")),
            P(("grp", "gx")),
        ),
        out_specs=P(None, None, ("grp", "gx"), None),
        check_vma=False,
    )
```
